32 devices in a mesh: node: 8 (over z, y), rep: 4 (over x, core).
Axes of the slice: x: 2, y: 2, z: 4, core: 2. Of those that a mesh axis runs over, the one named last changes fastest.
Arguments:
- features: bfloat16 [16384, 256], P('node'), may hold values from -6 to 6
- tiles: bfloat16 [8, 4, 4, 96, 128, 128], P('node', 'rep'), may hold values from -0.09375 to 0.09375
- tile_rows: int32 [8, 4, 4, 96], P('node', 'rep'), may hold values from 0 to 15
- tile_cols: int32 [8, 4, 4, 96], P('node', 'rep'), may hold values from 0 to 15
- tile_count: int32 [8, 4, 4], P('node', 'rep'), may hold values from 1 to 96, as said below
- order: int32 [16384], P('node'), may hold values from 0 to 16383, as said below
- weight: bfloat16 [256, 256], replicated, may hold values from -0.375 to 0.375
- cotangent: bfloat16 [16384, 256], P(('node', 'rep')), may hold values from -6 to 6
Outputs:
- activated: bfloat16 [16384, 256], P(('node', 'rep'))
- feature_grad: bfloat16 [16384, 256], P(('node', 'rep'))
- weight_grad: float32 [256, 256], replicated
The draws below stay inside these ranges and needn't reach their ends.
Inputs may be any that keep to these rules, and one draw needn't show every extreme that they name: `tile_count`: for every node block and offset, exactly one tile group holds 96 live slots; the counts of the others lie between 1 and 32. order is a permutation of the nodes that maps each aligned block of 512 positions onto itself.
All inputs are finite; a program needn't handle non-finite values.
Results may differ from the reference program's by a relative error of at most 0.017.
Values may be sent and summed in bfloat16 or wider, within the bound.
A program may use at most 128 MiB of HBM per device.

```python
import math
import jax
import jax.numpy as jnp
from jax import lax

F = 256
TILE = 128
CAPK = 96
BLOCKS = 8
REPS = 4
RB = 16
QROWS = 512
NODES = 16384


def draw_tile_count(key, part):
    first_key = jax.random.fold_in(key, 11)
    second_key = jax.random.fold_in(key, 23)
    base_count = jax.random.randint(first_key, (BLOCKS, REPS, 4), 1, max(2, CAPK // 3 + 1))
    busy_rep = jax.random.randint(second_key, (BLOCKS, 1, 4), 0, REPS)
    rep_ids = jnp.arange(REPS, dtype=jnp.int32)[None, :, None]
    return jnp.where(rep_ids == busy_rep, CAPK, base_count).astype(jnp.int32)


def draw_order(key, part):
    first_key = jax.random.fold_in(key, 37)
    block_count = NODES // QROWS
    scores = jax.random.randint(first_key, (block_count, QROWS), 0, 2 ** 30)
    within = jnp.argsort(scores, axis=1).astype(jnp.int32)
    starts = (jnp.arange(block_count, dtype=jnp.int32) * QROWS)[:, None]
    return (within + starts).reshape(NODES).astype(jnp.int32)


def touch_ends(entries, key, smallest, largest):
    spot = [jax.random.randint(jax.random.fold_in(key, axis), (), 0, length) for axis, length in enumerate(entries.shape)]
    widest = entries.shape.index(max(entries.shape))
    neighbour = spot[:widest] + [(spot[widest] + 1) % entries.shape[widest]] + spot[widest + 1:]
    return entries.at[tuple(spot)].set(smallest).at[tuple(neighbour)].set(largest)


def levels(key, extent, split, low, high):
    def one(dim, shards_of):
        draws = jax.random.uniform(jax.random.fold_in(jax.random.fold_in(key, 6), dim), (shards_of,), jnp.float32, low / len(split), high / len(split))
        return jnp.repeat(jnp.exp(draws), extent[dim] // shards_of).reshape((-1,) + (1,) * (len(extent) - dim - 1))

    factor_of = one(*split[0])
    for cut in split[1:]:
        factor_of = factor_of * one(*cut)
    return factor_of


def scatter_about(rng, shape, scale, bound, shards=(), kind=jnp.bfloat16):
    result = jax.random.normal(rng, shape, jnp.float32) * scale
    if len(shards) > 0:
        result = levels(rng, shape, shards, -0.22, 0.18) * result
    return jnp.clip(result, min=-bound, max=bound).astype(kind)


def setup_inputs(seed: int = 0) -> dict:
    seeds = jax.random.split(jax.random.key(seed), 9)
    features = scatter_about(seeds[0], (NODES, F), 1.0, 6.0, ((0, 8),))
    tiles = scatter_about(seeds[1], (BLOCKS, REPS, 4, CAPK, TILE, TILE), (6 * CAPK * TILE // RB) ** -0.5, 0.09375, ((0, 8), (1, 4)))
    tile_rows = touch_ends(jax.random.randint(seeds[2], (BLOCKS, REPS, 4, CAPK), 0, RB), jax.random.fold_in(seeds[2], 1), 0, RB - 1).astype(jnp.int32)
    tile_cols = touch_ends(jax.random.randint(seeds[3], (BLOCKS, REPS, 4, CAPK), 0, RB), jax.random.fold_in(seeds[3], 1), 0, RB - 1).astype(jnp.int32)
    tile_count = draw_tile_count(jax.random.fold_in(seeds[8], 71), 0)
    order = draw_order(jax.random.fold_in(seeds[8], 71), 0)
    weight = scatter_about(seeds[6], (F, F), F ** -0.5, 0.375)
    cotangent = scatter_about(seeds[7], (NODES, F), 1.0, 6.0, ((0, 32),))
    return {"features": features, "tiles": tiles, "tile_rows": tile_rows, "tile_cols": tile_cols, "tile_count": tile_count, "order": order, "weight": weight, "cotangent": cotangent}


def reference(features, tiles, tile_rows, tile_cols, tile_count, order, weight, cotangent):
    feat_width = features.shape[1]
    reordered = features[order]
    blocks = reordered.reshape(BLOCKS, RB, TILE, feat_width)
    slot_ids = jnp.arange(CAPK, dtype=jnp.int32)

    def masked(block_id, offset):
        live_mask = (slot_ids[None, :] < tile_count[block_id, :, offset][:, None]).astype(jnp.float32)
        return tiles[block_id, :, offset].astype(jnp.float32) * live_mask[:, :, None, None]

    def forward_block(block_id):
        totals = jnp.zeros((RB, TILE, feat_width), jnp.float32)
        for offset in range(4):
            source = blocks[(block_id + 1 - offset) % BLOCKS]
            gathered = source[tile_cols[block_id, :, offset]].astype(jnp.float32)
            products = jnp.einsum('rcab,rcbf->rcaf', masked(block_id, offset), gathered)
            totals = totals.at[tile_rows[block_id, :, offset].reshape(-1)].add(products.reshape(-1, TILE, feat_width))
        return totals
    aggregate = lax.map(forward_block, jnp.arange(BLOCKS, dtype=jnp.int32)).reshape(NODES, feat_width).astype(jnp.bfloat16)
    pre_act = jnp.dot(aggregate, weight, preferred_element_type=jnp.float32)
    gate_val = jax.nn.sigmoid(pre_act)
    activated = (pre_act * gate_val).astype(jnp.bfloat16)
    pre_grad = (cotangent.astype(jnp.float32) * gate_val * (1.0 + pre_act * (1.0 - gate_val))).astype(jnp.bfloat16)
    weight_grad = jnp.dot(aggregate.T, pre_grad, preferred_element_type=jnp.float32) * (1.0 / math.sqrt(NODES))
    back_rows = jnp.dot(pre_grad, weight.T, preferred_element_type=jnp.float32).astype(jnp.bfloat16)
    back_blocks = back_rows.reshape(BLOCKS, RB, TILE, feat_width)

    def backward_block(block_id):
        totals = jnp.zeros((RB, TILE, feat_width), jnp.float32)
        for offset in range(4):
            owner = (block_id - 1 + offset) % BLOCKS
            gathered = back_blocks[owner][tile_rows[owner, :, offset]].astype(jnp.float32)
            products = jnp.einsum('rcab,rcaf->rcbf', masked(owner, offset), gathered)
            totals = totals.at[tile_cols[owner, :, offset].reshape(-1)].add(products.reshape(-1, TILE, feat_width))
        return totals
    reordered_grad = lax.map(backward_block, jnp.arange(BLOCKS, dtype=jnp.int32)).reshape(NODES, feat_width)
    feature_grad = jnp.zeros((NODES, feat_width), jnp.float32).at[order].set(reordered_grad).astype(jnp.bfloat16)
    return (activated, feature_grad, weight_grad)
```

```python
import functools
import math

import jax
import jax.numpy as jnp
from jax import lax
from jax.experimental import pallas as pl
from jax.experimental.pallas import tpu as pltpu
from jax.sharding import PartitionSpec as P

CHUNK = 8
GROUP = 4


def from_behind(block, axis, distance):
    n = lax.axis_size(axis)
    return lax.ppermute(block, axis, [((i - distance) % n, i) for i in range(n)])


def stream(tiles, held, sems, count_ref, ks, step):
    chunks = tiles.shape[1] // CHUNK

    def copy(j, c):
        return pltpu.make_async_copy(
            tiles.at[ks[j], pl.ds(c * CHUNK, CHUNK)],
            held.at[j, pl.ds(c * CHUNK, CHUNK)],
            sems.at[j * chunks + c],
        )

    for j, k in enumerate(ks):
        live = lax.div(count_ref[k] + (CHUNK - 1), CHUNK)

        def begin(c, _, j=j):
            copy(j, c).start()
            return 0

        lax.fori_loop(0, live, begin, 0)
    for j, k in enumerate(ks):
        before, body, after = step(j, k)
        before()
        full = lax.div(count_ref[k], CHUNK)
        rest = count_ref[k] - full * CHUNK

        def whole(c, _, j=j):
            copy(j, c).wait()
            for g in range(0, CHUNK, GROUP):
                body([c * CHUNK + g + i for i in range(GROUP)])
            return 0

        lax.fori_loop(0, full, whole, 0)

        @pl.when(rest > 0)
        def _(j=j):
            copy(j, full).wait()

            def one(s, _):
                body([full * CHUNK + s])
                return 0

            lax.fori_loop(0, rest, one, 0)

        after()


def forward_kernel(ks, capacity, seeded, *refs):
    if seeded:
        count_ref, row_ref, col_ref, tiles, source, seed, out, held, acc, sems = refs
    else:
        count_ref, row_ref, col_ref, tiles, source, out, held, acc, sems = refs
    per = source.shape[2]
    if seeded:
        acc[...] = seed[...]
    else:
        acc[...] = jnp.zeros_like(acc)

    def step(j, k):
        def body(slots):
            products, puts = [], []
            for s in slots:
                col = col_ref[k * capacity + s]
                puts.append(row_ref[k * capacity + s])
                products.append(
                    jnp.dot(
                        held[j, s],
                        source[lax.div(col, per), j, lax.rem(col, per)],
                        preferred_element_type=jnp.float32,
                    )
                )
            for put, product in zip(puts, products):
                acc[put] += product

        return (lambda: None), body, (lambda: None)

    stream(tiles, held, sems, count_ref, ks, step)
    out[...] = acc[...].astype(out.dtype)


def backward_kernel(ks, capacity, count_ref, row_ref, col_ref, tiles, source, out, held, acc, sems):
    per = out.shape[2]

    def step(j, k):
        def before():
            acc[...] = jnp.zeros_like(acc)

        def body(slots):
            products, puts = [], []
            for s in slots:
                puts.append(col_ref[k * capacity + s])
                products.append(
                    lax.dot_general(
                        held[j, s],
                        source[row_ref[k * capacity + s]],
                        (((0,), (0,)), ((), ())),
                        preferred_element_type=jnp.float32,
                    )
                )
            for put, product in zip(puts, products):
                acc[put] += product

        def after():
            for q in range(out.shape[0]):
                out[q, j] = acc[q * per : (q + 1) * per].astype(out.dtype)

        return before, body, after

    stream(tiles, held, sems, count_ref, ks, step)


def tile_call(kernel, ks, out_shape, out_dtype, acc_shape, args, tiles):
    capacity, size = tiles.shape[1], tiles.shape[-1]
    smem = pl.BlockSpec(memory_space=pltpu.SMEM)
    vmem = pl.BlockSpec(memory_space=pltpu.VMEM)
    return pl.pallas_call(
        kernel,
        out_shape=jax.ShapeDtypeStruct(out_shape, out_dtype),
        in_specs=[smem] * 3 + [pl.BlockSpec(memory_space=pl.ANY)] + [vmem] * (len(args) - 4),
        out_specs=vmem,
        scratch_shapes=[
            pltpu.VMEM((len(ks), capacity, size, size), tiles.dtype),
            pltpu.VMEM(acc_shape, jnp.float32),
            pltpu.SemaphoreType.DMA((len(ks) * (capacity // CHUNK),)),
        ],
        compiler_params=pltpu.CompilerParams(vmem_limit_bytes=60 * 1024 * 1024),
    )(*args)


def local(features, tiles, tile_rows, tile_cols, tile_count, order, weight, cotangent):
    rows_dev, feat = features.shape
    size = tiles.shape[-1]
    blocks = rows_dev // size
    quarter = cotangent.shape[0]
    reps = lax.axis_size("rep")
    per = blocks // reps
    rep_pos = lax.axis_index("rep")
    tile_set = tiles[0, 0]
    capacity = tile_set.shape[1]
    row_ids = tile_rows.reshape(-1)
    col_ids = tile_cols.reshape(-1)
    counts = tile_count.reshape(-1)

    within = (order % quarter).reshape(reps, quarter)
    spots = jnp.arange(quarter, dtype=jnp.int32)
    my_order = lax.dynamic_index_in_dim(within, rep_pos, 0, keepdims=False)
    my_pick = (my_order[:, None] == spots[None, :]).astype(jnp.bfloat16)
    my_features = lax.dynamic_slice_in_dim(features, rep_pos * quarter, quarter, 0)
    mine = jnp.dot(my_pick, my_features, preferred_element_type=jnp.float32).astype(jnp.bfloat16)
    halo = jnp.stack([from_behind(mine, "node", d) for d in (-1, 1, 2)])
    gathered = lax.all_gather(halo, "rep", axis=0)
    gathered = gathered.reshape(reps, 3, per, size, feat)

    pick = (within[:, :, None] == spots[None, None, :]).astype(jnp.bfloat16)
    here = jnp.einsum(
        "qpi,qif->qpf",
        pick,
        features.reshape(reps, quarter, feat),
        preferred_element_type=jnp.float32,
    ).astype(jnp.bfloat16)
    here = here.reshape(reps, 1, per, size, feat)

    acc_shape = (blocks, size, feat)
    scalars = (counts, row_ids, col_ids, tile_set)
    own = tile_call(
        functools.partial(forward_kernel, (1,), capacity, False),
        (1,), acc_shape, jnp.float32, acc_shape, scalars + (here,), tile_set,
    )
    partial_value = tile_call(
        functools.partial(forward_kernel, (0, 2, 3), capacity, True),
        (0, 2, 3), acc_shape, jnp.bfloat16, acc_shape, scalars + (gathered, own), tile_set,
    )
    aggregate = lax.psum_scatter(
        partial_value.reshape(rows_dev, feat), "rep", scatter_dimension=0, tiled=True
    )
    pre_act = jnp.dot(aggregate, weight, preferred_element_type=jnp.float32)
    gate_val = jax.nn.sigmoid(pre_act)
    activated = (pre_act * gate_val).astype(jnp.bfloat16)
    pre_grad = (
        cotangent.astype(jnp.float32) * gate_val * (1.0 + pre_act * (1.0 - gate_val))
    ).astype(jnp.bfloat16)
    back_rows = lax.dot_general(
        pre_grad, weight, (((1,), (1,)), ((), ())), preferred_element_type=jnp.float32
    ).astype(jnp.bfloat16)
    full_back = lax.all_gather(back_rows, "rep", axis=0, tiled=True).reshape(blocks, size, feat)
    weight_part = lax.dot_general(
        aggregate, pre_grad, (((0,), (0,)), ((), ())), preferred_element_type=jnp.float32
    )
    grad_scale = 1.0 / math.sqrt(rows_dev * lax.axis_size("node"))
    weight_grad = lax.psum(weight_part, ("node", "rep")) * grad_scale

    away = tile_call(
        functools.partial(backward_kernel, (0, 2, 3), capacity),
        (0, 2, 3), (reps, 3, per, size, feat), jnp.bfloat16, acc_shape, scalars + (full_back,), tile_set,
    )
    home = tile_call(
        functools.partial(backward_kernel, (1,), capacity),
        (1,), (reps, 1, per, size, feat), jnp.bfloat16, acc_shape, scalars + (full_back,), tile_set,
    )
    away = lax.psum_scatter(away.reshape(reps, 3 * quarter, feat), "rep", scatter_dimension=0)
    home = lax.psum_scatter(home.reshape(rows_dev, feat), "rep", scatter_dimension=0, tiled=True)
    away = away.reshape(3, quarter, feat)
    total = home.astype(jnp.float32)
    for j, d in enumerate((1, -1, -2)):
        total = total + from_behind(away[j], "node", d).astype(jnp.float32)
    feature_grad = lax.dot_general(
        my_pick, total.astype(jnp.bfloat16), (((0,), (0,)), ((), ())), preferred_element_type=jnp.float32
    ).astype(jnp.bfloat16)
    return (activated, feature_grad, weight_grad)


def solution(mesh):
    placed = (
        P("node", None),
        P("node", "rep", None, None, None, None),
        P("node", "rep", None, None),
        P("node", "rep", None, None),
        P("node", "rep", None),
        P("node"),
        P(),
        P(("node", "rep"), None),
    )
    return jax.shard_map(
        local,
        mesh=mesh,
        in_specs=placed,
        out_specs=(P(("node", "rep"), None), P(("node", "rep"), None), P()),
        check_vma=False,
    )
```

```python
import functools
import math

import jax
import jax.numpy as jnp
from jax import lax
from jax.experimental import pallas as pl
from jax.experimental.pallas import tpu as pltpu
from jax.sharding import PartitionSpec as P

CHUNK = 8
GROUP = 4


def from_behind(block, axis, distance):
    n = lax.axis_size(axis)
    return lax.ppermute(block, axis, [((i - distance) % n, i) for i in range(n)])


def stream(tiles, held, sems, count_ref, ks, step):
    chunks = tiles.shape[1] // CHUNK

    def copy(j, c):
        return pltpu.make_async_copy(
            tiles.at[ks[j], pl.ds(c * CHUNK, CHUNK)],
            held.at[j, pl.ds(c * CHUNK, CHUNK)],
            sems.at[j * chunks + c],
        )

    for j, k in enumerate(ks):
        live = lax.div(count_ref[k] + (CHUNK - 1), CHUNK)

        def begin(c, _, j=j):
            copy(j, c).start()
            return 0

        lax.fori_loop(0, live, begin, 0)
    for j, k in enumerate(ks):
        before, body, after = step(j, k)
        before()
        full = lax.div(count_ref[k], CHUNK)
        rest = count_ref[k] - full * CHUNK

        def whole(c, _, j=j):
            copy(j, c).wait()
            for g in range(0, CHUNK, GROUP):
                body([c * CHUNK + g + i for i in range(GROUP)])
            return 0

        lax.fori_loop(0, full, whole, 0)

        @pl.when(rest > 0)
        def _(j=j):
            copy(j, full).wait()

            def one(s, _):
                body([full * CHUNK + s])
                return 0

            lax.fori_loop(0, rest, one, 0)

        after()


def forward_kernel(ks, capacity, seeded, *refs):
    if seeded:
        count_ref, row_ref, col_ref, tiles, source, seed, out, held, acc, sems = refs
    else:
        count_ref, row_ref, col_ref, tiles, source, out, held, acc, sems = refs
    per = source.shape[2]
    if seeded:
        acc[...] = seed[...]
    else:
        acc[...] = jnp.zeros_like(acc)

    def step(j, k):
        def body(slots):
            products, puts = [], []
            for s in slots:
                col = col_ref[k * capacity + s]
                puts.append(row_ref[k * capacity + s])
                products.append(
                    jnp.dot(
                        held[j, s],
                        source[lax.div(col, per), j, lax.rem(col, per)],
                        preferred_element_type=jnp.float32,
                    )
                )
            for put, product in zip(puts, products):
                acc[put] += product

        return (lambda: None), body, (lambda: None)

    stream(tiles, held, sems, count_ref, ks, step)
    out[...] = acc[...].astype(out.dtype)


def backward_kernel(ks, capacity, count_ref, row_ref, col_ref, tiles, source, out, held, acc, sems):
    per = out.shape[2]

    def step(j, k):
        def before():
            acc[...] = jnp.zeros_like(acc)

        def body(slots):
            products, puts = [], []
            for s in slots:
                puts.append(col_ref[k * capacity + s])
                products.append(
                    lax.dot_general(
                        held[j, s],
                        source[row_ref[k * capacity + s]],
                        (((0,), (0,)), ((), ())),
                        preferred_element_type=jnp.float32,
                    )
                )
            for put, product in zip(puts, products):
                acc[put] += product

        def after():
            for q in range(out.shape[0]):
                out[q, j] = acc[q * per : (q + 1) * per].astype(out.dtype)

        return before, body, after

    stream(tiles, held, sems, count_ref, ks, step)


def tile_call(kernel, ks, out_shape, out_dtype, acc_shape, args, tiles):
    capacity, size = tiles.shape[1], tiles.shape[-1]
    smem = pl.BlockSpec(memory_space=pltpu.SMEM)
    vmem = pl.BlockSpec(memory_space=pltpu.VMEM)
    return pl.pallas_call(
        kernel,
        out_shape=jax.ShapeDtypeStruct(out_shape, out_dtype),
        in_specs=[smem] * 3 + [pl.BlockSpec(memory_space=pl.ANY)] + [vmem] * (len(args) - 4),
        out_specs=vmem,
        scratch_shapes=[
            pltpu.VMEM((len(ks), capacity, size, size), tiles.dtype),
            pltpu.VMEM(acc_shape, jnp.float32),
            pltpu.SemaphoreType.DMA((len(ks) * (capacity // CHUNK),)),
        ],
        compiler_params=pltpu.CompilerParams(vmem_limit_bytes=60 * 1024 * 1024),
    )(*args)


def hop(src, dst, send, recv, axis, target):
    copy = pltpu.make_async_remote_copy(
        src_ref=src,
        dst_ref=dst,
        send_sem=send,
        recv_sem=recv,
        device_id={axis: target},
        device_id_type=pl.DeviceIdType.MESH,
    )
    copy.start()
    return copy


def greet(peers):
    barrier = pltpu.get_barrier_semaphore()
    for axis, target in peers:
        pl.semaphore_signal(
            barrier, inc=1, device_id={axis: target}, device_id_type=pl.DeviceIdType.MESH
        )
    pl.semaphore_wait(barrier, len(peers))


def dense_kernel(part, cot, weight, act, wpart, back, near, outgoing, far, full, send, recv):
    me = lax.axis_index("rep")
    x, c = me // 2, me % 2
    ox, oc = 1 - x, 1 - c
    sib, across, diag = x * 2 + oc, ox * 2 + c, ox * 2 + oc
    greet([("rep", sib), ("rep", across)])
    first = hop(part.at[diag], near.at[0], send.at[0], recv.at[0], "rep", sib)
    second = hop(part.at[sib], near.at[1], send.at[1], recv.at[1], "rep", sib)
    first.wait()
    outgoing[...] = (part[across].astype(jnp.float32) + near[0].astype(jnp.float32)).astype(
        outgoing.dtype
    )
    third = hop(outgoing, far, send.at[2], recv.at[2], "rep", across)
    second.wait()
    mine = part[me].astype(jnp.float32) + near[1].astype(jnp.float32)
    third.wait()
    aggregate = (mine + far[...].astype(jnp.float32)).astype(jnp.bfloat16)
    pre_act = jnp.dot(aggregate, weight[...], preferred_element_type=jnp.float32)
    gate = jax.nn.sigmoid(pre_act)
    act[...] = (pre_act * gate).astype(act.dtype)
    pre_grad = (
        cot[...].astype(jnp.float32) * gate * (1.0 + pre_act * (1.0 - gate))
    ).astype(jnp.bfloat16)
    full[me] = lax.dot_general(
        pre_grad, weight[...], (((1,), (1,)), ((), ())), preferred_element_type=jnp.float32
    ).astype(full.dtype)
    over = hop(full.at[me], full.at[me], send.at[3], recv.at[3], "rep", across)
    side = hop(full.at[me], full.at[me], send.at[4], recv.at[4], "rep", sib)
    wpart[...] = lax.dot_general(
        aggregate, pre_grad, (((0,), (0,)), ((), ())), preferred_element_type=jnp.float32
    )
    over.wait()
    relay = hop(full.at[across], full.at[across], send.at[5], recv.at[5], "rep", sib)
    side.wait()
    relay.wait()
    back[...] = full[...]


def sum_kernel(nodes, reps, scale, part, out, from_rep, held, from_node, full, rs, rr, ns, nr, gs, gr, os, orr):
    me, here = lax.axis_index("rep"), lax.axis_index("node")
    rep_peers = [(me + d) % reps for d in range(1, reps)]
    node_peers = [(here + d) % nodes for d in range(1, nodes)]
    greet([("rep", p) for p in rep_peers] + [("node", p) for p in node_peers])
    copies = [
        hop(part.at[p], from_rep.at[i], rs.at[i], rr.at[i], "rep", p)
        for i, p in enumerate(rep_peers)
    ]
    for copy in copies:
        copy.wait()
    total = part[me]
    for i in range(reps - 1):
        total = total + from_rep[i]
    held[...] = total
    copies = [
        hop(held.at[p], from_node.at[i], ns.at[i], nr.at[i], "node", p)
        for i, p in enumerate(node_peers)
    ]
    for copy in copies:
        copy.wait()
    total = held[here]
    for i in range(nodes - 1):
        total = total + from_node[i]
    full[me, here] = total * scale
    copies = [
        hop(full.at[me, here], full.at[me, here], gs.at[i], gr.at[i], "node", p)
        for i, p in enumerate(node_peers)
    ]
    for copy in copies:
        copy.wait()
    copies = [
        hop(full.at[me], full.at[me], os.at[i], orr.at[i], "rep", p)
        for i, p in enumerate(rep_peers)
    ]
    for copy in copies:
        copy.wait()
    out[...] = full[...]


def comm_params(ident):
    return pltpu.CompilerParams(
        collective_id=ident, has_side_effects=True, vmem_limit_bytes=60 * 1024 * 1024
    )


def dense_call(part, cot, weight):
    reps, rows, feat = part.shape
    vmem = pl.BlockSpec(memory_space=pltpu.VMEM)
    half = (rows, feat)
    return pl.pallas_call(
        dense_kernel,
        out_shape=(
            jax.ShapeDtypeStruct(half, jnp.bfloat16),
            jax.ShapeDtypeStruct((feat, feat), jnp.float32),
            jax.ShapeDtypeStruct(part.shape, jnp.bfloat16),
        ),
        in_specs=[vmem] * 3,
        out_specs=(vmem,) * 3,
        scratch_shapes=[
            pltpu.VMEM((2,) + half, jnp.bfloat16),
            pltpu.VMEM(half, jnp.bfloat16),
            pltpu.VMEM(half, jnp.bfloat16),
            pltpu.VMEM(part.shape, jnp.bfloat16),
            pltpu.SemaphoreType.DMA((6,)),
            pltpu.SemaphoreType.DMA((6,)),
        ],
        compiler_params=comm_params(0),
    )(part, cot, weight)


def sum_call(part, scale):
    nodes, reps = lax.axis_size("node"), lax.axis_size("rep")
    rows = part.size // (nodes * reps * 128)
    shape = (reps, nodes, rows, 128)
    vmem = pl.BlockSpec(memory_space=pltpu.VMEM)
    sems = [pltpu.SemaphoreType.DMA((n - 1,)) for n in (reps, reps, nodes, nodes, nodes, nodes, reps, reps)]
    out = pl.pallas_call(
        functools.partial(sum_kernel, nodes, reps, scale),
        out_shape=jax.ShapeDtypeStruct(shape, jnp.float32),
        in_specs=[vmem],
        out_specs=vmem,
        scratch_shapes=[
            pltpu.VMEM((reps - 1, nodes, rows, 128), jnp.float32),
            pltpu.VMEM((nodes, rows, 128), jnp.float32),
            pltpu.VMEM((nodes - 1, rows, 128), jnp.float32),
            pltpu.VMEM(shape, jnp.float32),
        ]
        + sems,
        compiler_params=comm_params(1),
    )(part.reshape(shape))
    return out.reshape(part.shape)


def local(features, tiles, tile_rows, tile_cols, tile_count, order, weight, cotangent):
    rows_dev, feat = features.shape
    size = tiles.shape[-1]
    blocks = rows_dev // size
    quarter = cotangent.shape[0]
    reps = lax.axis_size("rep")
    per = blocks // reps
    rep_pos = lax.axis_index("rep")
    tile_set = tiles[0, 0]
    capacity = tile_set.shape[1]
    row_ids = tile_rows.reshape(-1)
    col_ids = tile_cols.reshape(-1)
    counts = tile_count.reshape(-1)

    within = (order % quarter).reshape(reps, quarter)
    spots = jnp.arange(quarter, dtype=jnp.int32)
    my_order = lax.dynamic_index_in_dim(within, rep_pos, 0, keepdims=False)
    my_pick = (my_order[:, None] == spots[None, :]).astype(jnp.bfloat16)
    my_features = lax.dynamic_slice_in_dim(features, rep_pos * quarter, quarter, 0)
    mine = jnp.dot(my_pick, my_features, preferred_element_type=jnp.float32).astype(jnp.bfloat16)
    halo = jnp.stack([from_behind(mine, "node", d) for d in (-1, 1, 2)])
    gathered = lax.all_gather(halo, "rep", axis=0)
    gathered = gathered.reshape(reps, 3, per, size, feat)

    pick = (within[:, :, None] == spots[None, None, :]).astype(jnp.bfloat16)
    here = jnp.einsum(
        "qpi,qif->qpf",
        pick,
        features.reshape(reps, quarter, feat),
        preferred_element_type=jnp.float32,
    ).astype(jnp.bfloat16)
    here = here.reshape(reps, 1, per, size, feat)

    acc_shape = (blocks, size, feat)
    scalars = (counts, row_ids, col_ids, tile_set)
    own = tile_call(
        functools.partial(forward_kernel, (1,), capacity, False),
        (1,), acc_shape, jnp.float32, acc_shape, scalars + (here,), tile_set,
    )
    partial_value = tile_call(
        functools.partial(forward_kernel, (0, 2, 3), capacity, True),
        (0, 2, 3), acc_shape, jnp.bfloat16, acc_shape, scalars + (gathered, own), tile_set,
    )
    activated, weight_part, full_back = dense_call(
        partial_value.reshape(reps, quarter, feat), cotangent, weight
    )
    full_back = full_back.reshape(blocks, size, feat)
    grad_scale = 1.0 / math.sqrt(rows_dev * lax.axis_size("node"))
    weight_grad = sum_call(weight_part, grad_scale)

    away = tile_call(
        functools.partial(backward_kernel, (0, 2, 3), capacity),
        (0, 2, 3), (reps, 3, per, size, feat), jnp.bfloat16, acc_shape, scalars + (full_back,), tile_set,
    )
    home = tile_call(
        functools.partial(backward_kernel, (1,), capacity),
        (1,), (reps, 1, per, size, feat), jnp.bfloat16, acc_shape, scalars + (full_back,), tile_set,
    )
    away = lax.psum_scatter(away.reshape(reps, 3 * quarter, feat), "rep", scatter_dimension=0)
    home = lax.psum_scatter(home.reshape(rows_dev, feat), "rep", scatter_dimension=0, tiled=True)
    away = away.reshape(3, quarter, feat)
    total = home.astype(jnp.float32)
    for j, d in enumerate((1, -1, -2)):
        total = total + from_behind(away[j], "node", d).astype(jnp.float32)
    feature_grad = lax.dot_general(
        my_pick, total.astype(jnp.bfloat16), (((0,), (0,)), ((), ())), preferred_element_type=jnp.float32
    ).astype(jnp.bfloat16)
    return (activated, feature_grad, weight_grad)


def solution(mesh):
    placed = (
        P("node", None),
        P("node", "rep", None, None, None, None),
        P("node", "rep", None, None),
        P("node", "rep", None, None),
        P("node", "rep", None),
        P("node"),
        P(),
        P(("node", "rep"), None),
    )
    return jax.shard_map(
        local,
        mesh=mesh,
        in_specs=placed,
        out_specs=(P(("node", "rep"), None), P(("node", "rep"), None), P()),
        check_vma=False,
    )
```

```python
import functools
import math

import jax
import jax.numpy as jnp
from jax import lax
from jax.experimental import pallas as pl
from jax.experimental.pallas import tpu as pltpu
from jax.sharding import PartitionSpec as P

CHUNK = 8
GROUP = 4


def stream(tiles, held, sems, count_ref, ks, step):
    chunks = tiles.shape[1] // CHUNK

    def copy(j, c):
        return pltpu.make_async_copy(
            tiles.at[ks[j], pl.ds(c * CHUNK, CHUNK)],
            held.at[j, pl.ds(c * CHUNK, CHUNK)],
            sems.at[j * chunks + c],
        )

    for j, k in enumerate(ks):
        live = lax.div(count_ref[k] + (CHUNK - 1), CHUNK)

        def begin(c, _, j=j):
            copy(j, c).start()
            return 0

        lax.fori_loop(0, live, begin, 0)
    for j, k in enumerate(ks):
        before, body, after = step(j, k)
        before()
        full = lax.div(count_ref[k], CHUNK)
        rest = count_ref[k] - full * CHUNK

        def whole(c, _, j=j):
            copy(j, c).wait()
            for g in range(0, CHUNK, GROUP):
                body([c * CHUNK + g + i for i in range(GROUP)])
            return 0

        lax.fori_loop(0, full, whole, 0)

        @pl.when(rest > 0)
        def _(j=j):
            copy(j, full).wait()

            def one(s, _):
                body([full * CHUNK + s])
                return 0

            lax.fori_loop(0, rest, one, 0)

        after()


def forward_kernel(ks, capacity, seeded, *refs):
    if seeded:
        count_ref, row_ref, col_ref, tiles, source, seed, out, held, acc, sems = refs
    else:
        count_ref, row_ref, col_ref, tiles, source, out, held, acc, sems = refs
    per = source.shape[2]
    if seeded:
        acc[...] = seed[...]
    else:
        acc[...] = jnp.zeros_like(acc)

    def step(j, k):
        def body(slots):
            products, puts = [], []
            for s in slots:
                col = col_ref[k * capacity + s]
                puts.append(row_ref[k * capacity + s])
                products.append(
                    jnp.dot(
                        held[j, s],
                        source[lax.div(col, per), j, lax.rem(col, per)],
                        preferred_element_type=jnp.float32,
                    )
                )
            for put, product in zip(puts, products):
                acc[put] += product

        return (lambda: None), body, (lambda: None)

    stream(tiles, held, sems, count_ref, ks, step)
    out[...] = acc[...].astype(out.dtype)


def backward_kernel(ks, capacity, count_ref, row_ref, col_ref, tiles, source, out, held, acc, sems):
    per = out.shape[2]

    def step(j, k):
        def before():
            acc[...] = jnp.zeros_like(acc)

        def body(slots):
            products, puts = [], []
            for s in slots:
                puts.append(col_ref[k * capacity + s])
                products.append(
                    lax.dot_general(
                        held[j, s],
                        source[row_ref[k * capacity + s]],
                        (((0,), (0,)), ((), ())),
                        preferred_element_type=jnp.float32,
                    )
                )
            for put, product in zip(puts, products):
                acc[put] += product

        def after():
            for q in range(out.shape[0]):
                out[q, j] = acc[q * per : (q + 1) * per].astype(out.dtype)

        return before, body, after

    stream(tiles, held, sems, count_ref, ks, step)


def tile_call(kernel, ks, out_shape, out_dtype, acc_shape, args, tiles):
    capacity, size = tiles.shape[1], tiles.shape[-1]
    smem = pl.BlockSpec(memory_space=pltpu.SMEM)
    vmem = pl.BlockSpec(memory_space=pltpu.VMEM)
    return pl.pallas_call(
        kernel,
        out_shape=jax.ShapeDtypeStruct(out_shape, out_dtype),
        in_specs=[smem] * 3 + [pl.BlockSpec(memory_space=pl.ANY)] + [vmem] * (len(args) - 4),
        out_specs=vmem,
        scratch_shapes=[
            pltpu.VMEM((len(ks), capacity, size, size), tiles.dtype),
            pltpu.VMEM(acc_shape, jnp.float32),
            pltpu.SemaphoreType.DMA((len(ks) * (capacity // CHUNK),)),
        ],
        compiler_params=pltpu.CompilerParams(vmem_limit_bytes=60 * 1024 * 1024),
    )(*args)


def hop(src, dst, send, recv, axis, target):
    copy = pltpu.make_async_remote_copy(
        src_ref=src,
        dst_ref=dst,
        send_sem=send,
        recv_sem=recv,
        device_id={axis: target},
        device_id_type=pl.DeviceIdType.MESH,
    )
    copy.start()
    return copy


def greet(peers):
    barrier = pltpu.get_barrier_semaphore()
    for axis, target in peers:
        pl.semaphore_signal(
            barrier, inc=1, device_id={axis: target}, device_id_type=pl.DeviceIdType.MESH
        )
    pl.semaphore_wait(barrier, len(peers))


def dense_kernel(part, cot, weight, act, wpart, back, near, outgoing, far, full, send, recv):
    me = lax.axis_index("rep")
    x, c = me // 2, me % 2
    ox, oc = 1 - x, 1 - c
    sib, across, diag = x * 2 + oc, ox * 2 + c, ox * 2 + oc
    greet([("rep", sib), ("rep", across)])
    first = hop(part.at[diag], near.at[0], send.at[0], recv.at[0], "rep", sib)
    second = hop(part.at[sib], near.at[1], send.at[1], recv.at[1], "rep", sib)
    first.wait()
    outgoing[...] = (part[across].astype(jnp.float32) + near[0].astype(jnp.float32)).astype(
        outgoing.dtype
    )
    third = hop(outgoing, far, send.at[2], recv.at[2], "rep", across)
    second.wait()
    mine = part[me].astype(jnp.float32) + near[1].astype(jnp.float32)
    third.wait()
    aggregate = (mine + far[...].astype(jnp.float32)).astype(jnp.bfloat16)
    pre_act = jnp.dot(aggregate, weight[...], preferred_element_type=jnp.float32)
    gate = jax.nn.sigmoid(pre_act)
    act[...] = (pre_act * gate).astype(act.dtype)
    pre_grad = (
        cot[...].astype(jnp.float32) * gate * (1.0 + pre_act * (1.0 - gate))
    ).astype(jnp.bfloat16)
    full[me] = lax.dot_general(
        pre_grad, weight[...], (((1,), (1,)), ((), ())), preferred_element_type=jnp.float32
    ).astype(full.dtype)
    over = hop(full.at[me], full.at[me], send.at[3], recv.at[3], "rep", across)
    side = hop(full.at[me], full.at[me], send.at[4], recv.at[4], "rep", sib)
    wpart[...] = lax.dot_general(
        aggregate, pre_grad, (((0,), (0,)), ((), ())), preferred_element_type=jnp.float32
    )
    over.wait()
    relay = hop(full.at[across], full.at[across], send.at[5], recv.at[5], "rep", sib)
    side.wait()
    relay.wait()
    back[...] = full[...]


def halo_kernel(nodes, mine, out, full, send, recv):
    me, here = lax.axis_index("rep"), lax.axis_index("node")
    x, c = me // 2, me % 2
    sib, across = x * 2 + 1 - c, (1 - x) * 2 + c
    greet(
        [("rep", sib), ("rep", across)]
        + [("node", (here + d) % nodes) for d in (1, nodes - 1, 2, nodes - 2)]
    )
    arrivals = [
        hop(mine, full.at[me, j], send.at[j], recv.at[j], "node", (here + d) % nodes)
        for j, d in enumerate((nodes - 1, 1, 2))
    ]
    over, rest = [], []
    for j in range(3):
        arrivals[j].wait()
        own = full.at[me, j]
        over.append(hop(own, own, send.at[3 + j], recv.at[3 + j], "rep", across))
        rest.append(hop(own, own, send.at[6 + j], recv.at[6 + j], "rep", sib))
    for j in range(3):
        over[j].wait()
        other = full.at[across, j]
        rest.append(hop(other, other, send.at[9 + j], recv.at[9 + j], "rep", sib))
    for copy in rest:
        copy.wait()
    out[...] = full[...]


def halo_call(mine, reps):
    shape = (reps, 3) + mine.shape
    vmem = pl.BlockSpec(memory_space=pltpu.VMEM)
    return pl.pallas_call(
        functools.partial(halo_kernel, lax.axis_size("node")),
        out_shape=jax.ShapeDtypeStruct(shape, mine.dtype),
        in_specs=[vmem],
        out_specs=vmem,
        scratch_shapes=[
            pltpu.VMEM(shape, mine.dtype),
            pltpu.SemaphoreType.DMA((12,)),
            pltpu.SemaphoreType.DMA((12,)),
        ],
        compiler_params=comm_params(2),
    )(mine)


def finish_kernel(
    nodes, reps, scale, terms, pick, part, grad, out,
    near, outgoing, far, leaving, got, total, from_rep, held, from_node, full,
    send, recv, rs, rr, ns, nr, gs, gr, os, orr,
):
    me, here = lax.axis_index("rep"), lax.axis_index("node")
    x, c = me // 2, me % 2
    sib, across, diag = x * 2 + 1 - c, (1 - x) * 2 + c, (1 - x) * 2 + 1 - c
    rep_peers = [(me + d) % reps for d in range(1, reps)]
    node_peers = [(here + d) % nodes for d in range(1, nodes)]
    greet([("rep", p) for p in rep_peers] + [("node", p) for p in node_peers])
    first = [
        hop(terms.at[diag, j], near.at[0, j], send.at[j], recv.at[j], "rep", sib)
        for j in range(4)
    ]
    second = [
        hop(terms.at[sib, j], near.at[1, j], send.at[4 + j], recv.at[4 + j], "rep", sib)
        for j in range(4)
    ]
    to_reps = [
        hop(part.at[p], from_rep.at[i], rs.at[i], rr.at[i], "rep", p)
        for i, p in enumerate(rep_peers)
    ]
    third = []
    for j in range(4):
        first[j].wait()
        outgoing[j] = (
            terms[across, j].astype(jnp.float32) + near[0, j].astype(jnp.float32)
        ).astype(outgoing.dtype)
        third.append(hop(outgoing.at[j], far.at[j], send.at[8 + j], recv.at[8 + j], "rep", across))
    for copy in to_reps:
        copy.wait()
    share = part[me]
    for i in range(reps - 1):
        share = share + from_rep[i]
    held[...] = share
    to_nodes = [
        hop(held.at[p], from_node.at[i], ns.at[i], nr.at[i], "node", p)
        for i, p in enumerate(node_peers)
    ]
    fourth = []
    for j, d in enumerate((1, nodes - 1, nodes - 2, 0)):
        second[j].wait()
        third[j].wait()
        value = (
            terms[me, j].astype(jnp.float32)
            + near[1, j].astype(jnp.float32)
            + far[j].astype(jnp.float32)
        )
        if d:
            leaving[j] = value.astype(leaving.dtype)
            fourth.append(
                hop(leaving.at[j], got.at[j], send.at[12 + j], recv.at[12 + j], "node", (here + d) % nodes)
            )
        else:
            total[...] = value
    for copy in to_nodes:
        copy.wait()
    share = held[here]
    for i in range(nodes - 1):
        share = share + from_node[i]
    full[me, here] = share * scale
    spread = [
        hop(full.at[me, here], full.at[me, here], gs.at[i], gr.at[i], "node", p)
        for i, p in enumerate(node_peers)
    ]
    for copy in spread:
        copy.wait()
    gather = [
        hop(full.at[me], full.at[me], os.at[i], orr.at[i], "rep", p)
        for i, p in enumerate(rep_peers)
    ]
    for copy in fourth:
        copy.wait()
    value = total[...]
    for j in range(3):
        value = value + got[j].astype(jnp.float32)
    grad[...] = lax.dot_general(
        pick[...], value.astype(jnp.bfloat16), (((0,), (0,)), ((), ())), preferred_element_type=jnp.float32
    ).astype(grad.dtype)
    for copy in gather:
        copy.wait()
    out[...] = full[...]


def finish_call(terms, pick, part, scale):
    nodes, reps = lax.axis_size("node"), lax.axis_size("rep")
    rows = part.size // (nodes * reps * 128)
    shape = (reps, nodes, rows, 128)
    block = terms.shape[2:]
    vmem = pl.BlockSpec(memory_space=pltpu.VMEM)
    sems = [
        pltpu.SemaphoreType.DMA((n,))
        for n in (15, 15) + (reps - 1,) * 2 + (nodes - 1,) * 4 + (reps - 1,) * 2
    ]
    grad, out = pl.pallas_call(
        functools.partial(finish_kernel, nodes, reps, scale),
        out_shape=(
            jax.ShapeDtypeStruct(block, jnp.bfloat16),
            jax.ShapeDtypeStruct(shape, jnp.float32),
        ),
        in_specs=[vmem] * 3,
        out_specs=(vmem,) * 2,
        scratch_shapes=[
            pltpu.VMEM((2, 4) + block, jnp.bfloat16),
            pltpu.VMEM((4,) + block, jnp.bfloat16),
            pltpu.VMEM((4,) + block, jnp.bfloat16),
            pltpu.VMEM((3,) + block, jnp.bfloat16),
            pltpu.VMEM((3,) + block, jnp.bfloat16),
            pltpu.VMEM(block, jnp.float32),
            pltpu.VMEM((reps - 1, nodes, rows, 128), jnp.float32),
            pltpu.VMEM((nodes, rows, 128), jnp.float32),
            pltpu.VMEM((nodes - 1, rows, 128), jnp.float32),
            pltpu.VMEM(shape, jnp.float32),
        ]
        + sems,
        compiler_params=comm_params(1),
    )(terms, pick, part.reshape(shape))
    return grad, out.reshape(part.shape)


def comm_params(ident):
    return pltpu.CompilerParams(
        collective_id=ident, has_side_effects=True, vmem_limit_bytes=60 * 1024 * 1024
    )


def dense_call(part, cot, weight):
    reps, rows, feat = part.shape
    vmem = pl.BlockSpec(memory_space=pltpu.VMEM)
    half = (rows, feat)
    return pl.pallas_call(
        dense_kernel,
        out_shape=(
            jax.ShapeDtypeStruct(half, jnp.bfloat16),
            jax.ShapeDtypeStruct((feat, feat), jnp.float32),
            jax.ShapeDtypeStruct(part.shape, jnp.bfloat16),
        ),
        in_specs=[vmem] * 3,
        out_specs=(vmem,) * 3,
        scratch_shapes=[
            pltpu.VMEM((2,) + half, jnp.bfloat16),
            pltpu.VMEM(half, jnp.bfloat16),
            pltpu.VMEM(half, jnp.bfloat16),
            pltpu.VMEM(part.shape, jnp.bfloat16),
            pltpu.SemaphoreType.DMA((6,)),
            pltpu.SemaphoreType.DMA((6,)),
        ],
        compiler_params=comm_params(0),
    )(part, cot, weight)


def local(features, tiles, tile_rows, tile_cols, tile_count, order, weight, cotangent):
    rows_dev, feat = features.shape
    size = tiles.shape[-1]
    blocks = rows_dev // size
    quarter = cotangent.shape[0]
    reps = lax.axis_size("rep")
    per = blocks // reps
    rep_pos = lax.axis_index("rep")
    tile_set = tiles[0, 0]
    capacity = tile_set.shape[1]
    row_ids = tile_rows.reshape(-1)
    col_ids = tile_cols.reshape(-1)
    counts = tile_count.reshape(-1)

    within = (order % quarter).reshape(reps, quarter)
    spots = jnp.arange(quarter, dtype=jnp.int32)
    my_order = lax.dynamic_index_in_dim(within, rep_pos, 0, keepdims=False)
    my_pick = (my_order[:, None] == spots[None, :]).astype(jnp.bfloat16)
    my_features = lax.dynamic_slice_in_dim(features, rep_pos * quarter, quarter, 0)
    mine = jnp.dot(my_pick, my_features, preferred_element_type=jnp.float32).astype(jnp.bfloat16)
    gathered = halo_call(mine, reps)
    gathered = gathered.reshape(reps, 3, per, size, feat)

    pick = (within[:, :, None] == spots[None, None, :]).astype(jnp.bfloat16)
    here = jnp.einsum(
        "qpi,qif->qpf",
        pick,
        features.reshape(reps, quarter, feat),
        preferred_element_type=jnp.float32,
    ).astype(jnp.bfloat16)
    here = here.reshape(reps, 1, per, size, feat)

    acc_shape = (blocks, size, feat)
    scalars = (counts, row_ids, col_ids, tile_set)
    own = tile_call(
        functools.partial(forward_kernel, (1,), capacity, False),
        (1,), acc_shape, jnp.float32, acc_shape, scalars + (here,), tile_set,
    )
    partial_value = tile_call(
        functools.partial(forward_kernel, (0, 2, 3), capacity, True),
        (0, 2, 3), acc_shape, jnp.bfloat16, acc_shape, scalars + (gathered, own), tile_set,
    )
    activated, weight_part, full_back = dense_call(
        partial_value.reshape(reps, quarter, feat), cotangent, weight
    )
    full_back = full_back.reshape(blocks, size, feat)
    grad_scale = 1.0 / math.sqrt(rows_dev * lax.axis_size("node"))
    terms = tile_call(
        functools.partial(backward_kernel, (0, 2, 3, 1), capacity),
        (0, 2, 3, 1), (reps, 4, per, size, feat), jnp.bfloat16, acc_shape, scalars + (full_back,), tile_set,
    )
    feature_grad, weight_grad = finish_call(
        terms.reshape(reps, 4, quarter, feat), my_pick, weight_part, grad_scale
    )
    return (activated, feature_grad, weight_grad)


def solution(mesh):
    placed = (
        P("node", None),
        P("node", "rep", None, None, None, None),
        P("node", "rep", None, None),
        P("node", "rep", None, None),
        P("node", "rep", None),
        P("node"),
        P(),
        P(("node", "rep"), None),
    )
    return jax.shard_map(
        local,
        mesh=mesh,
        in_specs=placed,
        out_specs=(P(("node", "rep"), None), P(("node", "rep"), None), P()),
        check_vma=False,
    )
```
